32 devices in a mesh: groups: 2 (over y), frames: 4 (over x, core), bands: 4 (over z).
Axes of the slice: x: 2, y: 2, z: 4, core: 2. Of those that a mesh axis runs over, the one named last changes fastest.
Arguments:
- span_tokens: bfloat16 [8, 64, 3072], P(('groups', 'frames')), parts along dimension 0, may hold values from -6 to 6
- w_query: bfloat16 [3072, 3072], P(None, 'bands'), may hold values from -0.109375 to 0.109375
- w_key: bfloat16 [3072, 3072], P(None, 'bands'), may hold values from -0.109375 to 0.109375
- w_value: bfloat16 [3072, 3072], P(None, 'bands'), may hold values from -0.109375 to 0.109375
- cache_keys: bfloat16 [128, 64, 3072], P(('groups', 'frames'), None, 'bands'), parts along dimension 0
- cache_values: bfloat16 [128, 64, 3072], P(('groups', 'frames'), None, 'bands'), parts along dimension 0, may hold values from -6 to 6
- frame_counts: int32 [128], P(('groups', 'frames')), parts along dimension 0, may hold values from 8 to 64, as said below
- rollback_start: int32 [2], P('groups'), parts along dimension 0, may hold values from 32 to 64
- w_proj: bfloat16 [3072, 128], P('bands'), may hold values from -0.109375 to 0.109375
- norm_gain: float32 [128], replicated, may hold values from 0.5 to 2
- conv_first: bfloat16 [3, 3, 3, 128, 128], replicated, may hold values from -0.109375 to 0.109375
- bias_first: float32 [128], replicated, may hold values from -3 to 3
- conv_second: bfloat16 [3, 3, 3, 128, 128], replicated, may hold values from -0.109375 to 0.109375
- bias_second: float32 [128], replicated, may hold values from -3 to 3
Outputs:
- decoded: bfloat16 [8, 16, 16, 128], P(('groups', 'frames'), 'bands'), parts along dimension 0
The draws below stay inside these ranges and needn't reach their ends.
There are 2 independent parts, one for each index of `groups`. The reference program is written for one: setup_inputs(seed, part) draws one part's arguments, and reference() takes and returns one part's arrays. A program takes and returns all parts, laid end to end along the dimension named above; an argument that names none is the same for every part. Nothing has to cross between parts.
Inputs may be any that keep to these rules, and one draw needn't show every extreme that they name: `frame_counts`: some frame has exactly 64 valid tokens and some exactly max(8, 1).
All inputs are finite; a program needn't handle non-finite values.
Results may differ from the reference program's by a relative error of at most 0.014.
Values may be sent and summed in bfloat16 or wider, within the bound.
A program may use at most 128 MiB of HBM per device.

```python
import math
import jax
import jax.numpy as jnp
from jax import lax

D = 3072
HEADS = 24
HD = 128
C = 128
HT = 8
WT = 8
FR_DEV = 16
FT = 64
CACHE_FR = 64
CF = 4
QTOK = 256
N_FRAMES = 4


def draw_cache_keys(key, part):
    base = jax.random.normal(jax.random.fold_in(key, 11), (CACHE_FR, FT, D), jnp.float32)
    return base.astype(jnp.bfloat16)


def draw_frame_counts(key, part):
    lowest = max(FT // 8, 1)
    counts = jax.random.randint(jax.random.fold_in(key, 21), (CACHE_FR,), lowest, FT + 1)
    first = jax.random.randint(jax.random.fold_in(key, 22), (), 0, CACHE_FR)
    second = (first + 1 + jax.random.randint(jax.random.fold_in(key, 23), (), 0, CACHE_FR - 1)) % CACHE_FR
    places = jnp.arange(CACHE_FR)
    counts = jnp.where(places == first, FT, counts)
    counts = jnp.where(places == second, lowest, counts)
    return counts.astype(jnp.int32)


def steps_of(key, dims, shards, smallest, top_value):
    loudness = 1.0
    for axis_at, blocks in shards:
        heights = jax.random.uniform(jax.random.fold_in(jax.random.fold_in(key, 6), axis_at), (blocks,), jnp.float32, smallest / len(shards), top_value / len(shards))
        loudness = loudness * jnp.repeat(jnp.exp(heights), dims[axis_at] // blocks).reshape((-1,) + (1,) * (len(dims) - 1 - axis_at))
    return loudness


def gaussian(key, extent, scale, bound, cuts=(), kind=jnp.bfloat16):
    drawn = jax.random.normal(key, extent, jnp.float32) * scale
    if len(cuts) > 0:
        drawn = steps_of(key, extent, cuts, -0.22, 0.18) * drawn
    return jnp.clip(drawn, min=-bound, max=bound).astype(kind)


def setup_inputs(seed: int = 0, part: int = 0) -> dict:
    key_of = jax.random.split(jax.random.key(seed), 15)
    own_keys = jax.random.split(jax.random.fold_in(key_of[14], part), 15)
    return {
        "span_tokens": gaussian(own_keys[0], (CF, FT, D), 1.0, 6.0, ((0, 4),)),
        "w_query": gaussian(key_of[1], (D, D), D ** -0.5, 0.109375, ((1, 4),)),
        "w_key": gaussian(key_of[2], (D, D), D ** -0.5, 0.109375, ((1, 4),)),
        "w_value": gaussian(key_of[3], (D, D), D ** -0.5, 0.109375, ((1, 4),)),
        "cache_keys": draw_cache_keys(jax.random.fold_in(jax.random.fold_in(key_of[14], part), 71), part),
        "cache_values": gaussian(own_keys[5], (CACHE_FR, FT, D), 1.0, 6.0, ((0, 4), (2, 4))),
        "frame_counts": draw_frame_counts(jax.random.fold_in(jax.random.fold_in(key_of[14], part), 71), part),
        "rollback_start": jax.random.randint(own_keys[7], (1,), CACHE_FR // 2, CACHE_FR + 1).astype(jnp.int32),
        "w_proj": gaussian(key_of[8], (D, C), D ** -0.5, 0.109375, ((0, 4),)),
        "norm_gain": jnp.clip(jnp.exp(jax.random.uniform(key_of[9], (C,), jnp.float32, math.log(0.5), math.log(2.0))), 0.5, 2.0),
        "conv_first": gaussian(key_of[10], (3, 3, 3, C, C), (27 * C) ** -0.5, 0.109375),
        "bias_first": gaussian(key_of[11], (C,), 0.5, 3.0, (), jnp.float32),
        "conv_second": gaussian(key_of[12], (3, 3, 3, C, C), (27 * C) ** -0.5, 0.109375),
        "bias_second": gaussian(key_of[13], (C,), 0.5, 3.0, (), jnp.float32),
    }


def causal_conv(field, weight, bias):
    frames_n, rows_n, cols_n = (field.shape[0], field.shape[1], field.shape[2])
    padded = jnp.pad(field, ((2, 0), (1, 1), (1, 1), (0, 0))).astype(jnp.float32)
    total = jnp.zeros((frames_n, rows_n, cols_n, weight.shape[-1]), jnp.float32)
    for shift_t in range(3):
        for shift_y in range(3):
            for shift_x in range(3):
                window = padded[shift_t:shift_t + frames_n, shift_y:shift_y + rows_n, shift_x:shift_x + cols_n]
                total = total + jnp.einsum('thwc,cd->thwd', window, weight[shift_t, shift_y, shift_x].astype(jnp.float32))
    return total + bias

def reference(span_tokens, w_query, w_key, w_value, cache_keys, cache_values, frame_counts, rollback_start, w_proj, norm_gain, conv_first, bias_first, conv_second, bias_second):
    flat = span_tokens.reshape(QTOK, D)
    queries = jnp.dot(flat, w_query, preferred_element_type=jnp.float32).astype(jnp.bfloat16)
    new_keys = jnp.dot(flat, w_key, preferred_element_type=jnp.float32).astype(jnp.bfloat16).reshape(CF, FT, D)
    new_values = jnp.dot(flat, w_value, preferred_element_type=jnp.float32).astype(jnp.bfloat16).reshape(CF, FT, D)
    query_frame = jnp.arange(QTOK, dtype=jnp.int32) // FT
    key_slot = jnp.arange(FR_DEV * FT, dtype=jnp.int32)
    query_heads = queries.astype(jnp.float32).reshape(QTOK, HEADS, HD)

    def partials(block_index):
        first = block_index * FR_DEV
        cached_k = lax.dynamic_slice_in_dim(cache_keys, first, FR_DEV, 0).reshape(FR_DEV * FT, D)
        cached_v = lax.dynamic_slice_in_dim(cache_values, first, FR_DEV, 0).reshape(FR_DEV * FT, D)
        own_counts = lax.dynamic_slice_in_dim(frame_counts, first, FR_DEV, 0)
        visible_cache = (first + key_slot // FT < rollback_start[0]) & (key_slot % FT < jnp.repeat(own_counts, FT))
        all_keys = jnp.concatenate([cached_k, lax.dynamic_index_in_dim(new_keys, block_index, 0, keepdims=False)], 0)
        all_values = jnp.concatenate([cached_v, lax.dynamic_index_in_dim(new_values, block_index, 0, keepdims=False)], 0)
        all_keys = all_keys.astype(jnp.float32).reshape(-1, HEADS, HD)
        all_values = all_values.astype(jnp.float32).reshape(-1, HEADS, HD)
        visible = jnp.concatenate([jnp.broadcast_to(visible_cache[None, :], (QTOK, FR_DEV * FT)), jnp.broadcast_to((query_frame >= block_index)[:, None], (QTOK, FT))], 1)
        scores = jnp.einsum('qhd,khd->hqk', query_heads, all_keys) * HD ** (-0.5)
        scores = jnp.where(visible[None], scores, -1e+30)
        maxima = lax.optimization_barrier(jnp.max(scores, -1))
        weights = jnp.where(visible[None], jnp.exp(scores - maxima[..., None]), 0.0).astype(jnp.bfloat16)
        totals = lax.optimization_barrier(jnp.sum(weights.astype(jnp.float32), -1))
        outputs = jnp.einsum('hqk,khd->qhd', weights.astype(jnp.float32), all_values)
        return (maxima, totals, outputs)
    maxima, totals, outputs = lax.map(partials, jnp.arange(N_FRAMES, dtype=jnp.int32))
    top = lax.optimization_barrier(jnp.max(maxima, 0))
    factor = jnp.exp(maxima - top[None])
    total = lax.optimization_barrier(jnp.sum(factor * totals, 0))
    combined = lax.optimization_barrier(jnp.sum(outputs * jnp.transpose(factor, (0, 2, 1))[..., None], 0))
    attended = (combined / jnp.transpose(total)[..., None]).reshape(QTOK, D).astype(jnp.bfloat16)
    latent = jnp.dot(attended, w_proj, preferred_element_type=jnp.float32).astype(jnp.bfloat16).reshape(CF, HT, WT, C)
    latent_f = latent.astype(jnp.float32)
    mean_square = lax.optimization_barrier(jnp.mean(latent_f * latent_f, -1, keepdims=True))
    activated = jax.nn.silu(latent_f * lax.rsqrt(mean_square + 1e-06) * norm_gain).astype(jnp.bfloat16)
    hidden = (latent_f + causal_conv(activated, conv_first, bias_first)).astype(jnp.bfloat16)
    upsampled = jnp.repeat(jnp.repeat(hidden, 2, axis=1), 2, axis=2)
    return causal_conv(upsampled, conv_second, bias_second).astype(jnp.bfloat16)
```

```python
import functools
import math

import jax
import jax.numpy as jnp
from jax import lax
from jax.experimental import pallas as pl
from jax.experimental.pallas import tpu as pltpu
from jax.sharding import PartitionSpec as P

HD = 128
WT = 8
AGES = 5
LATE = 2
MESH = pl.DeviceIdType.MESH
F32 = jnp.float32
BF16 = jnp.bfloat16
NEG = -1e30


def rolled(x, steps):
    rows = x.shape[0]
    column = lax.broadcasted_iota(jnp.int32, x.shape, 0) % WT
    edge = 0 if steps == 1 else WT - 1
    return jnp.where(column == edge, 0.0, pltpu.roll(x, steps % rows, 0))


def kernel(
    frames_n,
    bands_n,
    counts_ref,
    start_ref,
    tokens_hbm,
    wq_hbm,
    wk_hbm,
    wv_hbm,
    keys_hbm,
    values_hbm,
    proj_hbm,
    gain_ref,
    conv1_hbm,
    bias1_ref,
    conv2_hbm,
    bias2_ref,
    out_ref,
    tok,
    wq,
    wk,
    wv,
    kbuf,
    vbuf,
    proj,
    conv1,
    conv2,
    qall,
    pbuf,
    obuf,
    rbuf,
    st_out,
    st_in,
    colbuf,
    part,
    ybuf,
    outf,
    in_sem,
    q_send,
    q_recv,
    o_send,
    o_recv,
    chain,
    st_send,
    st_recv,
    y_send,
    y_recv,
):
    f = lax.axis_index("frames")
    b = lax.axis_index("bands")
    slot_n = tok.shape[0]
    chunk_n, _, cw = wq.shape
    cached_n = counts_ref.shape[0]
    cached_rows = cached_n * slot_n
    heads = chunk_n * cw // HD
    part_rows = slot_n // bands_n
    band_rows = part_rows // WT
    reach = 2 // band_rows

    sem_i = [0]
    loads = {}

    def load(name, src, dst):
        copy = pltpu.make_async_copy(src, dst, in_sem.at[sem_i[0]])
        sem_i[0] += 1
        copy.start()
        loads[name] = copy

    load("tok", tokens_hbm, tok)
    for c in range(chunk_n):
        load(("q", c), wq_hbm.at[:, pl.ds(c * cw, cw)], wq.at[c])
    for c in range(chunk_n):
        load(("k", c), wk_hbm.at[:, pl.ds(c * cw, cw)], wk.at[c])
    load("keys", keys_hbm, kbuf.at[pl.ds(0, cached_rows)])
    for c in range(chunk_n):
        load(("v", c), wv_hbm.at[:, pl.ds(c * cw, cw)], wv.at[c])
    load("values", values_hbm, vbuf.at[pl.ds(0, cached_rows)])
    load("proj", proj_hbm, proj)
    load("conv1", conv1_hbm, conv1)
    load("conv2", conv2_hbm, conv2)

    ybuf[...] = jnp.zeros_like(ybuf)
    barrier = pltpu.get_barrier_semaphore()

    def greet(i, carry):
        pl.semaphore_signal(
            barrier,
            inc=1,
            device_id={"frames": lax.rem(f + i, frames_n)},
            device_id_type=MESH,
        )
        return carry

    lax.fori_loop(1, frames_n, greet, 0)

    def beside(sem, step):
        pl.semaphore_signal(sem, inc=1, device_id={"bands": b + step}, device_id_type=MESH)

    @pl.when(b > 0)
    def _():
        beside(barrier, -1)

    @pl.when(b < bands_n - 1)
    def _():
        beside(barrier, 1)

    greeted = frames_n - 1 + (b > 0).astype(jnp.int32) + (b < bands_n - 1).astype(jnp.int32)

    def relay_entry(step):
        if step > 0:

            @pl.when(b == step)
            def _():
                pl.semaphore_wait(chain.at[0], 1)

            @pl.when(b == bands_n - 1 - step)
            def _():
                pl.semaphore_wait(chain.at[1], 1)

        if step < bands_n - 1:

            @pl.when(b == step)
            def _():
                beside(chain.at[0], 1)

            @pl.when(b == bands_n - 1 - step)
            def _():
                beside(chain.at[1], -1)

    pad_rows = kbuf.shape[0] - cached_rows - slot_n
    kbuf[pl.ds(cached_rows + slot_n, pad_rows), :] = jnp.zeros((pad_rows, kbuf.shape[1]), BF16)
    vbuf[pl.ds(cached_rows + slot_n, pad_rows), :] = jnp.zeros((pad_rows, kbuf.shape[1]), BF16)

    pending = []

    share = 2 if frames_n % 2 == 0 else 1
    core = lax.rem(f, share)
    node = f // share
    nodes = frames_n // share
    q_block = share * slot_n
    others = [(dn, dc) for dn in range(nodes) for dc in range(share) if (dn, dc) != (0, 0)]
    far = [(dn, dc) for dn, dc in others if dn > 0]
    near = [(dn, dc) for dn, dc in others if dn == 0]

    def node_at(dn):
        return lax.rem(node + dn, nodes)

    def peer(dn, dc):
        return node_at(dn) * share + (1 - core if dc else core)

    def source_of(dn, dc):
        return peer(nodes - dn, dc)

    def remote(src, dst, send, recv, target, begin=True):
        copy = pltpu.make_async_remote_copy(
            src_ref=src,
            dst_ref=dst,
            send_sem=send,
            recv_sem=recv,
            device_id={"frames": target},
            device_id_type=MESH,
        )
        if begin:
            copy.start()
            pending.append(copy)
        return copy

    def query_copy(c, way, begin):
        target = peer(*way) if begin else source_of(*way)
        i = way[0] * share + way[1]
        rows = qall.at[c, f if begin else target]
        return remote(rows, rows, q_send.at[c, i], q_recv.at[c, i], target, begin)

    def output_copy(h, way, begin):
        target = peer(*way) if begin else source_of(*way)
        i = way[0] * share + way[1]
        dst = rbuf.at[f if begin else target, h]
        return remote(obuf.at[target, h], dst, o_send.at[i, h], o_recv.at[i, h], target, begin)

    def stats_copy(way, begin):
        target = peer(*way) if begin else source_of(*way)
        i = way[0] * share + way[1]
        src = st_out.at[target // share]
        dst = st_in.at[f if begin else target]
        return remote(src, dst, st_send.at[i], st_recv.at[i], target, begin)

    loads["tok"].wait()
    scale = HD ** (-0.5) * math.log2(math.e)
    for c in range(chunk_n):
        loads[("q", c)].wait()
        queries = jnp.dot(tok[...], wq[c], preferred_element_type=F32) * scale
        qall[c, f] = queries.astype(BF16)
        if c == 0:
            pl.semaphore_wait(barrier, greeted)
        for way in far + near:
            query_copy(c, way, True)
    relay_entry(0)
    for c in range(chunk_n):
        loads[("k", c)].wait()
        kbuf[pl.ds(cached_rows, slot_n), pl.ds(c * cw, cw)] = jnp.dot(
            tok[...], wk[c], preferred_element_type=F32
        ).astype(BF16)
    if bands_n > 1:
        relay_entry(1)
    for c in range(chunk_n):
        loads[("v", c)].wait()
        vbuf[pl.ds(cached_rows, slot_n), pl.ds(c * cw, cw)] = jnp.dot(
            tok[...], wv[c], preferred_element_type=F32
        ).astype(BF16)
    if bands_n > 2:
        relay_entry(2)

    lane = lax.broadcasted_iota(jnp.int32, (1, HD), 1)
    per_tile = HD // slot_n
    bias_tiles = []
    for tile in range(cached_rows // HD):
        visible = lane < 0
        for s in range(per_tile):
            g = tile * per_tile + s
            slot = lane - s * slot_n
            shown = (slot >= 0) & (slot < counts_ref[g]) & (slot < slot_n)
            visible = visible | (shown & ((lane * 0 + (f * cached_n + g)) < start_ref[0]))
        bias_tiles.append(jnp.where(visible, 0.0, NEG))
    bias_row = jnp.concatenate(bias_tiles, 1)

    row = lax.broadcasted_iota(jnp.int32, (q_block, HD), 0)
    wide_lane = lax.broadcasted_iota(jnp.int32, (q_block, HD), 1)

    loads["keys"].wait()
    loads["values"].wait()

    def weigh(h, base):
        q = qall[h * HD // cw, pl.ds(base, share), :, pl.ds(h * HD % cw, HD)]
        q = q.reshape(q_block, HD)
        k = kbuf[:, pl.ds(h * HD, HD)]
        raw = lax.dot_general(q, k, (((1,), (1,)), ((), ())), preferred_element_type=F32)
        old = raw[:, :cached_rows] + bias_row
        new = jnp.where(
            (wide_lane < slot_n) & (row + base * slot_n >= f * slot_n), raw[:, cached_rows:], NEG
        )
        top = jnp.maximum(jnp.max(old, 1, keepdims=True), jnp.max(new, 1, keepdims=True))
        w_old = jnp.exp2(old - top)
        w_new = jnp.exp2(new - top)
        total = jnp.sum(w_old, 1, keepdims=True) + jnp.sum(w_new, 1, keepdims=True)
        pbuf[h, :, pl.ds(0, cached_rows)] = w_old.astype(BF16)
        pbuf[h, :, pl.ds(cached_rows, HD)] = w_new.astype(BF16)
        return top, total

    def gather(h, base):
        out = jnp.dot(pbuf[h], vbuf[:, pl.ds(h * HD, HD)], preferred_element_type=F32)
        obuf[pl.ds(base, share), h] = out.astype(BF16).reshape(share, slot_n, HD)

    late = min(LATE, heads - 1)
    for dn in range(nodes):
        ways = near if dn == 0 else [way for way in far if way[0] == dn]
        block = node_at(dn)
        base = block * share
        stat = jnp.zeros((q_block, HD), F32)
        for h in range(heads):
            if h * HD % cw == 0:
                back = [((nodes - way[0]) % nodes, way[1]) for way in ways]
                for way in back:
                    query_copy(h * HD // cw, way, False).wait_recv()
            top, total = weigh(h, base)
            stat = jnp.where(wide_lane == h, top, stat)
            stat = jnp.where(wide_lane == 8 + h, total, stat)
            if h < heads - late:
                gather(h, base)
                for way in ways:
                    output_copy(h, way, True)
        st_out[block] = jnp.transpose(stat)[:16]
        for way in ways:
            stats_copy(way, True)
        for h in range(heads - late, heads):
            gather(h, base)
            for way in ways:
                output_copy(h, way, True)
        if dn == 0:
            rbuf[f] = obuf[f]
            st_in[f] = st_out[node]
            for step in range(3, bands_n):
                relay_entry(step)

    loads["proj"].wait()
    for way in others:
        stats_copy(way, False).wait_recv()
    top = st_in[0, :8]
    for k in range(1, frames_n):
        top = jnp.maximum(top, st_in[k, :8])
    parts = [jnp.exp2(st_in[k, :8] - top) for k in range(frames_n)]
    summed = jnp.zeros_like(top)
    for k in range(frames_n):
        summed += parts[k] * st_in[k, 8:16]
    head_row = lax.broadcasted_iota(jnp.int32, top.shape, 0)
    inverse = jnp.where(head_row < heads, 1.0 / summed, 0.0)
    factor = [part_k * inverse for part_k in parts]
    if frames_n * 8 < HD:
        factor.append(jnp.zeros((HD - frames_n * 8, q_block), F32))
    colbuf[...] = jnp.transpose(jnp.concatenate(factor, 0))
    column = colbuf[pl.ds(core * slot_n, slot_n), :]
    partial = jnp.zeros((slot_n, HD), F32)
    for c in range(chunk_n):
        attended = []
        for h in range(c * cw // HD, (c + 1) * cw // HD):
            for way in others:
                output_copy(h, way, False).wait_recv()
            mixed = jnp.zeros((slot_n, HD), F32)
            for k in range(frames_n):
                i = k * 8 + h
                mixed += rbuf[k, h].astype(F32) * column[:, i : i + 1]
            attended.append(mixed.astype(BF16))
        partial += jnp.dot(
            jnp.concatenate(attended, 1), proj[pl.ds(c * cw, cw), :], preferred_element_type=F32
        )
    part[...] = partial.astype(BF16).reshape(bands_n, part_rows, HD)

    width = min(2 * reach + 1, bands_n)
    offsets = [
        (age, e)
        for age in range(min(AGES, frames_n))
        for e in range(bands_n)
        if (age, e) != (0, 0)
    ]

    def hand(age, e, begin):
        other = lax.rem(b + (e if begin else bands_n - e), bands_n)
        goal = other if begin else b
        first = jnp.clip(goal - reach, 0, bands_n - width)
        return pltpu.make_async_remote_copy(
            src_ref=part.at[pl.ds(first, width)],
            dst_ref=ybuf.at[AGES - 1 - age, b if begin else other, pl.ds(first + reach, width)],
            send_sem=y_send.at[age, e],
            recv_sem=y_recv.at[age, e],
            device_id={"frames": lax.rem(f + age, frames_n), "bands": other},
            device_id_type=MESH,
        )

    def sends(age):
        return f + age < frames_n

    def takes(age):
        return f - age >= 0

    for age, e in sorted(offsets, key=lambda o: (-o[0], -o[1])):

        @pl.when(sends(age))
        def _(age=age, e=e):
            hand(age, e, True).start()

    ybuf[AGES - 1, b, pl.ds(reach, bands_n)] = part[...]
    loads["conv1"].wait()
    loads["conv2"].wait()
    for age, e in offsets:

        @pl.when(takes(age))
        def _(age=age, e=e):
            hand(age, e, False).wait_recv()

    latent = jnp.zeros((AGES, 2 * reach + 1, part_rows, HD), F32)
    for s in range(bands_n):
        latent += ybuf[:, s, pl.ds(b, 2 * reach + 1)].astype(F32)

    rows_in = band_rows + 4
    rows_mid = band_rows + 2
    latent = latent.astype(BF16).astype(F32).reshape(AGES, rows_in, WT, HD)
    flat = latent.reshape(AGES * rows_in * WT, HD)
    mean_square = jnp.mean(flat * flat, -1, keepdims=True)
    normed = flat * lax.rsqrt(mean_square + 1e-06) * gain_ref[...]
    active = (normed * jax.nn.sigmoid(normed)).astype(BF16).astype(F32)
    taps = jnp.concatenate([rolled(active, 1), active, rolled(active, -1)], 1)
    taps = taps.reshape(AGES, rows_in, WT, 3 * HD)
    mid = 3 * rows_mid * WT
    acc = jnp.zeros((mid, HD), F32)
    for i in range(3):
        for j in range(3):
            window = taps[i : i + 3, j : j + rows_mid].reshape(mid, 3 * HD).astype(BF16)
            acc += jnp.dot(window, conv1[i * 3 + j], preferred_element_type=F32)
    centre = latent[2:, 1 : 1 + rows_mid].reshape(mid, HD)
    index = lax.broadcasted_iota(jnp.int32, (mid, HD), 0)
    at_frame = index // (rows_mid * WT) + f - 2
    at_row = index // WT % rows_mid + b * band_rows - 1
    inside = (at_frame >= 0) & (at_row >= 0) & (at_row < bands_n * band_rows)
    hidden = jnp.where(inside, centre + (acc + bias1_ref[...]), 0.0).astype(BF16).astype(F32)
    left, right = rolled(hidden, 1), rolled(hidden, -1)
    sides = [
        jnp.concatenate(list(cols), 1).reshape(3, rows_mid, WT, 3 * HD)
        for cols in ((left, hidden, hidden), (hidden, hidden, right))
    ]
    out_rows = 2 * band_rows
    acc = jnp.zeros((2 * out_rows * WT, HD), F32)
    for i in range(3):
        for j in range(3):
            window = jnp.concatenate(
                [side[i, (y + j + 1) // 2] for side in sides for y in range(out_rows)], 0
            ).astype(BF16)
            acc += jnp.dot(window, conv2[i * 3 + j], preferred_element_type=F32)
    acc = acc + bias2_ref[...]
    for p in range(2):
        for y in range(out_rows):
            first = (p * out_rows + y) * WT
            outf[y, pl.ds(p, WT, 2), :] = acc[first : first + WT]
    out_ref[0] = outf[...].astype(BF16)

    for copy in pending:
        copy.wait_send()
    for age, e in offsets:

        @pl.when(sends(age))
        def _(age=age, e=e):
            hand(age, e, True).wait_send()


def local(
    frames_n,
    bands_n,
    span_tokens,
    w_query,
    w_key,
    w_value,
    cache_keys,
    cache_values,
    frame_counts,
    rollback_start,
    w_proj,
    norm_gain,
    conv_first,
    bias_first,
    conv_second,
    bias_second,
):
    _, slot_n, width = span_tokens.shape
    cached_n, _, lw = cache_keys.shape
    rows = cached_n * slot_n
    cw = 256 if lw % 256 == 0 else 128
    chunk_n = lw // cw
    heads = lw // HD
    share = 2 if frames_n % 2 == 0 else 1
    q_block = share * slot_n
    part_rows = slot_n // bands_n
    band_rows = part_rows // WT
    reach = 2 // band_rows
    key_rows = rows + HD
    anywhere = pl.BlockSpec(memory_space=pl.ANY)
    smem = pl.BlockSpec(memory_space=pltpu.SMEM)
    vmem = pl.BlockSpec(memory_space=pltpu.VMEM)
    dma = pltpu.SemaphoreType.DMA
    return pl.pallas_call(
        functools.partial(kernel, frames_n, bands_n),
        out_shape=pltpu.VMEM((1, 2 * band_rows, 2 * WT, HD), BF16),
        in_specs=[smem, smem] + [anywhere] * 7 + [vmem, anywhere, vmem, anywhere, vmem],
        out_specs=vmem,
        scratch_shapes=[
            pltpu.VMEM((slot_n, width), BF16),
            pltpu.VMEM((chunk_n, width, cw), BF16),
            pltpu.VMEM((chunk_n, width, cw), BF16),
            pltpu.VMEM((chunk_n, width, cw), BF16),
            pltpu.VMEM((key_rows, lw), BF16),
            pltpu.VMEM((key_rows, lw), BF16),
            pltpu.VMEM((lw, HD), BF16),
            pltpu.VMEM((9, 3 * HD, HD), BF16),
            pltpu.VMEM((9, 3 * HD, HD), BF16),
            pltpu.VMEM((chunk_n, frames_n, slot_n, cw), BF16),
            pltpu.VMEM((heads, q_block, key_rows), BF16),
            pltpu.VMEM((frames_n, heads, slot_n, HD), BF16),
            pltpu.VMEM((frames_n, heads, slot_n, HD), BF16),
            pltpu.VMEM((frames_n // share, 16, q_block), F32),
            pltpu.VMEM((frames_n, 16, q_block), F32),
            pltpu.VMEM((q_block, HD), F32),
            pltpu.VMEM((bands_n, part_rows, HD), BF16),
            pltpu.VMEM((AGES, bands_n, bands_n + 2 * reach, part_rows, HD), BF16),
            pltpu.VMEM((2 * band_rows, 2 * WT, HD), F32),
            dma((6 + 3 * chunk_n,)),
            dma((chunk_n, frames_n)),
            dma((chunk_n, frames_n)),
            dma((frames_n, heads)),
            dma((frames_n, heads)),
            pltpu.SemaphoreType.REGULAR((2,)),
            dma((frames_n,)),
            dma((frames_n,)),
            dma((AGES, bands_n)),
            dma((AGES, bands_n)),
        ],
        compiler_params=pltpu.CompilerParams(
            collective_id=0, has_side_effects=True, vmem_limit_bytes=60 * 1024 * 1024
        ),
    )(
        frame_counts,
        rollback_start,
        span_tokens.reshape(slot_n, width),
        w_query,
        w_key,
        w_value,
        cache_keys.reshape(rows, lw),
        cache_values.reshape(rows, lw),
        w_proj,
        norm_gain.reshape(1, HD),
        conv_first.reshape(9, 3 * HD, HD),
        bias_first.reshape(1, HD),
        conv_second.reshape(9, 3 * HD, HD),
        bias_second.reshape(1, HD),
    )


def solution(mesh):
    placed = (
        P(("groups", "frames"), None, None),
        P(None, "bands"),
        P(None, "bands"),
        P(None, "bands"),
        P(("groups", "frames"), None, "bands"),
        P(("groups", "frames"), None, "bands"),
        P(("groups", "frames")),
        P("groups"),
        P("bands", None),
        P(),
        P(),
        P(),
        P(),
        P(),
    )
    return jax.shard_map(
        functools.partial(local, mesh.shape["frames"], mesh.shape["bands"]),
        mesh=mesh,
        in_specs=placed,
        out_specs=P(("groups", "frames"), "bands", None, None),
        check_vma=False,
    )
```

```python
import functools
import math

import jax
import jax.numpy as jnp
from jax import lax
from jax.experimental import pallas as pl
from jax.experimental.pallas import tpu as pltpu
from jax.sharding import PartitionSpec as P

HD = 128
WT = 8
AGES = 5
MESH = pl.DeviceIdType.MESH
F32 = jnp.float32
BF16 = jnp.bfloat16
NEG = -1e30


def rolled(x, steps):
    rows = x.shape[0]
    column = lax.broadcasted_iota(jnp.int32, x.shape, 0) % WT
    edge = 0 if steps == 1 else WT - 1
    return jnp.where(column == edge, 0.0, pltpu.roll(x, steps % rows, 0))


def kernel(
    frames_n,
    bands_n,
    counts_ref,
    start_ref,
    tokens_hbm,
    wq_hbm,
    wk_hbm,
    wv_hbm,
    keys_hbm,
    values_hbm,
    proj_hbm,
    gain_ref,
    conv1_hbm,
    bias1_ref,
    conv2_hbm,
    bias2_ref,
    out_ref,
    tok,
    wq,
    wk,
    wv,
    kbuf,
    vbuf,
    proj,
    conv1,
    conv2,
    qall,
    pbuf,
    obuf,
    stats,
    part,
    rsbuf,
    lat,
    outf,
    in_sem,
    q_send,
    q_recv,
    pass_send,
    pass_recv,
    chain,
    st_send,
    st_recv,
    rs_send,
    rs_recv,
    ag_send,
    ag_recv,
):
    f = lax.axis_index("frames")
    b = lax.axis_index("bands")
    group_n = frames_n * bands_n
    me = f * bands_n + b
    slot_n = tok.shape[0]
    chunk_n, _, cw = wq.shape
    cached_n = counts_ref.shape[0]
    cached_rows = cached_n * slot_n
    heads = chunk_n * cw // HD
    q_total = frames_n * slot_n
    part_rows = slot_n // bands_n
    band_rows = part_rows // WT
    reach = 2 // band_rows

    sem_i = [0]
    loads = {}

    def load(name, src, dst):
        copy = pltpu.make_async_copy(src, dst, in_sem.at[sem_i[0]])
        sem_i[0] += 1
        copy.start()
        loads[name] = copy

    load("tok", tokens_hbm, tok)
    for c in range(chunk_n):
        load(("q", c), wq_hbm.at[:, pl.ds(c * cw, cw)], wq.at[c])
    for c in range(chunk_n):
        load(("k", c), wk_hbm.at[:, pl.ds(c * cw, cw)], wk.at[c])
    for c in range(chunk_n):
        load(("v", c), wv_hbm.at[:, pl.ds(c * cw, cw)], wv.at[c])
    load("keys", keys_hbm, kbuf.at[pl.ds(0, cached_rows)])
    load("values", values_hbm, vbuf.at[pl.ds(0, cached_rows)])
    load("proj", proj_hbm, proj)
    load("conv1", conv1_hbm, conv1)
    load("conv2", conv2_hbm, conv2)

    lat[...] = jnp.zeros_like(lat)
    barrier = pltpu.get_barrier_semaphore()

    def greet(i, carry):
        pl.semaphore_signal(
            barrier,
            inc=1,
            device_id={"frames": lax.rem(f + i, frames_n)},
            device_id_type=MESH,
        )
        return carry

    lax.fori_loop(1, frames_n, greet, 0)

    def beside(sem, step):
        pl.semaphore_signal(sem, inc=1, device_id={"bands": b + step}, device_id_type=MESH)

    @pl.when(b > 0)
    def _():
        beside(barrier, -1)

    @pl.when(b < bands_n - 1)
    def _():
        beside(barrier, 1)

    greeted = frames_n - 1 + (b > 0).astype(jnp.int32) + (b < bands_n - 1).astype(jnp.int32)

    def relay_entry(step):
        if step > 0:

            @pl.when(b == step)
            def _():
                pl.semaphore_wait(chain.at[0], 1)

            @pl.when(b == bands_n - 1 - step)
            def _():
                pl.semaphore_wait(chain.at[1], 1)

        if step < bands_n - 1:

            @pl.when(b == step)
            def _():
                beside(chain.at[0], 1)

            @pl.when(b == bands_n - 1 - step)
            def _():
                beside(chain.at[1], -1)

    pad_rows = kbuf.shape[0] - cached_rows - slot_n
    kbuf[pl.ds(cached_rows + slot_n, pad_rows), :] = jnp.zeros((pad_rows, kbuf.shape[1]), BF16)
    vbuf[pl.ds(cached_rows + slot_n, pad_rows), :] = jnp.zeros((pad_rows, kbuf.shape[1]), BF16)

    pending = []

    def remote(src, dst, send, recv, target, begin=True):
        copy = pltpu.make_async_remote_copy(
            src_ref=src,
            dst_ref=dst,
            send_sem=send,
            recv_sem=recv,
            device_id={"frames": target},
            device_id_type=MESH,
        )
        if begin:
            copy.start()
            pending.append(copy)
        return copy

    share = 2 if frames_n % 2 == 0 else 1
    core = lax.rem(f, share)
    node = f // share
    nodes = frames_n // share
    mate = f + 1 - 2 * core if share == 2 else f
    first = 0 if share == 2 else 1

    def query_copy(c, d, begin):
        step = d if begin else nodes - d
        target = lax.rem(node + step, nodes) * share + core if d > 0 else mate
        rows = qall.at[c, f if begin else target]
        return remote(rows, rows, q_send.at[c, d], q_recv.at[c, d], target, begin)

    def pass_copy(c, d, begin):
        source = lax.rem(node + nodes - d, nodes) * share
        rows = qall.at[c, source + (core if begin else 1 - core)]
        return remote(rows, rows, pass_send.at[c, d], pass_recv.at[c, d], mate, begin)

    def relay_queries(c):
        for d in range(1, nodes):
            query_copy(c, d, False).wait_recv()
            if share == 2:
                pass_copy(c, d, True)

    loads["tok"].wait()
    scale = HD ** (-0.5) * math.log2(math.e)
    for c in range(chunk_n):
        loads[("q", c)].wait()
        queries = jnp.dot(tok[...], wq[c], preferred_element_type=F32) * scale
        qall[c, f] = queries.astype(BF16)
        if c == 0:
            pl.semaphore_wait(barrier, greeted)
        for d in [*range(1, nodes), *range(first, 1)]:
            query_copy(c, d, True)
    relay_entry(0)
    for c in range(chunk_n):
        loads[("k", c)].wait()
        kbuf[pl.ds(cached_rows, slot_n), pl.ds(c * cw, cw)] = jnp.dot(
            tok[...], wk[c], preferred_element_type=F32
        ).astype(BF16)
    for c in range(chunk_n):
        loads[("v", c)].wait()
        vbuf[pl.ds(cached_rows, slot_n), pl.ds(c * cw, cw)] = jnp.dot(
            tok[...], wv[c], preferred_element_type=F32
        ).astype(BF16)
        relay_queries(c)
    if bands_n > 1:
        relay_entry(1)

    lane = lax.broadcasted_iota(jnp.int32, (1, HD), 1)
    per_tile = HD // slot_n
    bias_tiles = []
    for tile in range(cached_rows // HD):
        visible = lane < 0
        for s in range(per_tile):
            g = tile * per_tile + s
            slot = lane - s * slot_n
            shown = (slot >= 0) & (slot < counts_ref[g]) & (slot < slot_n)
            visible = visible | (shown & ((lane * 0 + (f * cached_n + g)) < start_ref[0]))
        bias_tiles.append(jnp.where(visible, 0.0, NEG))
    bias_row = jnp.concatenate(bias_tiles, 1)

    q_block = min(q_total, 256)
    row = lax.broadcasted_iota(jnp.int32, (q_block, HD), 0)
    wide_lane = lax.broadcasted_iota(jnp.int32, (q_block, HD), 1)

    loads["keys"].wait()
    loads["values"].wait()

    def settle(c):
        if share == 2:
            query_copy(c, 0, False).wait_recv()
            for d in range(1, nodes):
                pass_copy(c, d, False).wait_recv()

    def weigh(h, block):
        per = q_block // slot_n
        q = qall[h * HD // cw, pl.ds(block * per, per), :, pl.ds(h * HD % cw, HD)]
        q = q.reshape(q_block, HD)
        k = kbuf[:, pl.ds(h * HD, HD)]
        raw = lax.dot_general(q, k, (((1,), (1,)), ((), ())), preferred_element_type=F32)
        old = raw[:, :cached_rows] + bias_row
        new = jnp.where(
            (wide_lane < slot_n) & (row + block * q_block >= f * slot_n),
            raw[:, cached_rows:],
            NEG,
        )
        top = jnp.maximum(jnp.max(old, 1, keepdims=True), jnp.max(new, 1, keepdims=True))
        w_old = jnp.exp2(old - top)
        w_new = jnp.exp2(new - top)
        total = jnp.sum(w_old, 1, keepdims=True) + jnp.sum(w_new, 1, keepdims=True)
        pbuf[h, pl.ds(block * q_block, q_block), pl.ds(0, cached_rows)] = w_old.astype(BF16)
        pbuf[h, pl.ds(block * q_block, q_block), pl.ds(cached_rows, HD)] = w_new.astype(BF16)
        return top, total

    def gather(h, block):
        rows = pl.ds(block * q_block, q_block)
        obuf[h, rows, :] = jnp.dot(
            pbuf[h, rows, :], vbuf[:, pl.ds(h * HD, HD)], preferred_element_type=F32
        )

    blocks = range(q_total // q_block)
    late = min(4, heads - 1)
    for block in blocks:
        stat = jnp.zeros((q_block, HD), F32)
        for h in range(heads):
            if block == 0 and h * HD % cw == 0:
                settle(h * HD // cw)
            top, total = weigh(h, block)
            stat = jnp.where(wide_lane == h, top, stat)
            stat = jnp.where(wide_lane == 8 + h, total, stat)
            if h < heads - late:
                gather(h, block)
        stats[f, :, pl.ds(block * q_block, q_block)] = jnp.transpose(stat)[:16]
    if bands_n > 2:
        relay_entry(2)
    for d in range(1, frames_n):
        copy = pltpu.make_async_remote_copy(
            src_ref=stats.at[f],
            dst_ref=stats.at[f],
            send_sem=st_send.at[d],
            recv_sem=st_recv.at[d],
            device_id={"frames": lax.rem(f + d, frames_n)},
            device_id_type=MESH,
        )
        copy.start()
        pending.append(copy)
    for block in blocks:
        for h in range(heads - late, heads):
            gather(h, block)
    for d in range(1, frames_n):
        source = lax.rem(f + frames_n - d, frames_n)
        pltpu.make_async_remote_copy(
            src_ref=stats.at[source],
            dst_ref=stats.at[source],
            send_sem=st_send.at[d],
            recv_sem=st_recv.at[d],
            device_id={"frames": source},
            device_id_type=MESH,
        ).wait_recv()
    for step in range(3, bands_n):
        relay_entry(step)
    loads["proj"].wait()
    top = stats[0, :8]
    for k in range(1, frames_n):
        top = jnp.maximum(top, stats[k, :8])
    summed = jnp.zeros_like(top)
    for k in range(frames_n):
        summed += jnp.exp2(stats[k, :8] - top) * stats[k, 8:16]
    head_row = lax.broadcasted_iota(jnp.int32, top.shape, 0)
    factor = jnp.where(head_row < heads, jnp.exp2(stats[f, :8] - top) / summed, 0.0)
    factor = jnp.concatenate([factor, jnp.zeros((HD - 8, q_total), F32)], 0)
    for block in blocks:
        rows = pl.ds(block * q_block, q_block)
        column = jnp.transpose(factor[:, block * q_block : (block + 1) * q_block])
        scaled = jnp.concatenate(
            [(obuf[h, rows, :] * column[:, h : h + 1]).astype(BF16) for h in range(heads)], 1
        )
        partial = jnp.dot(scaled, proj[...], preferred_element_type=F32).astype(BF16)
        per = q_block // part_rows
        part[pl.ds(block * per, per)] = partial.reshape(per, part_rows, HD)

    def scatter(i, carry):
        other = lax.rem(me + i, group_n)
        pltpu.make_async_remote_copy(
            src_ref=part.at[other],
            dst_ref=rsbuf.at[me],
            send_sem=rs_send.at[i],
            recv_sem=rs_recv.at[i],
            device_id={"frames": other // bands_n, "bands": lax.rem(other, bands_n)},
            device_id_type=MESH,
        ).start()
        return carry

    lax.fori_loop(1, group_n, scatter, 0, unroll=group_n <= 16)
    rsbuf[me] = part[me]
    loads["conv1"].wait()
    loads["conv2"].wait()

    def received(i, carry):
        other = lax.rem(me + group_n - i, group_n)
        copy = pltpu.make_async_remote_copy(
            src_ref=part.at[other],
            dst_ref=rsbuf.at[other],
            send_sem=rs_send.at[i],
            recv_sem=rs_recv.at[i],
            device_id={"frames": other // bands_n, "bands": lax.rem(other, bands_n)},
            device_id_type=MESH,
        )
        copy.wait_recv()
        return carry

    lax.fori_loop(1, group_n, received, 0, unroll=group_n <= 16)
    own = jnp.sum(rsbuf[...].astype(F32), 0)
    lat[AGES - 1, reach] = own.astype(BF16)

    offsets = [
        (age, e)
        for age in range(min(AGES, frames_n))
        for e in range(-reach, reach + 1)
        if (age, e) != (0, 0)
    ]

    def hand(age, e):
        return pltpu.make_async_remote_copy(
            src_ref=lat.at[AGES - 1, reach],
            dst_ref=lat.at[AGES - 1 - age, reach - e],
            send_sem=ag_send.at[age, e + reach],
            recv_sem=ag_recv.at[age, e + reach],
            device_id={
                "frames": lax.rem(f + age, frames_n),
                "bands": lax.rem(b + e + bands_n, bands_n),
            },
            device_id_type=MESH,
        )

    def sends(age, e):
        return (f + age < frames_n) & (b + e >= 0) & (b + e < bands_n)

    def takes(age, e):
        return (f - age >= 0) & (b - e >= 0) & (b - e < bands_n)

    for age, e in offsets:

        @pl.when(sends(age, e))
        def _(age=age, e=e):
            hand(age, e).start()

    for age, e in offsets:

        @pl.when(takes(age, e))
        def _(age=age, e=e):
            hand(age, e).wait_recv()

    rows_in = band_rows + 4
    rows_mid = band_rows + 2
    latent = lat[...].astype(F32).reshape(AGES, rows_in, WT, HD)
    flat = latent.reshape(AGES * rows_in * WT, HD)
    mean_square = jnp.mean(flat * flat, -1, keepdims=True)
    normed = flat * lax.rsqrt(mean_square + 1e-06) * gain_ref[...]
    active = (normed * jax.nn.sigmoid(normed)).astype(BF16).astype(F32)
    taps = jnp.concatenate([rolled(active, 1), active, rolled(active, -1)], 1)
    taps = taps.reshape(AGES, rows_in, WT, 3 * HD)
    mid = 3 * rows_mid * WT
    acc = jnp.zeros((mid, HD), F32)
    for i in range(3):
        for j in range(3):
            window = taps[i : i + 3, j : j + rows_mid].reshape(mid, 3 * HD).astype(BF16)
            acc += jnp.dot(window, conv1[i * 3 + j], preferred_element_type=F32)
    centre = latent[2:, 1 : 1 + rows_mid].reshape(mid, HD)
    index = lax.broadcasted_iota(jnp.int32, (mid, HD), 0)
    at_frame = index // (rows_mid * WT) + f - 2
    at_row = index // WT % rows_mid + b * band_rows - 1
    inside = (at_frame >= 0) & (at_row >= 0) & (at_row < bands_n * band_rows)
    hidden = jnp.where(inside, centre + (acc + bias1_ref[...]), 0.0).astype(BF16).astype(F32)
    left, right = rolled(hidden, 1), rolled(hidden, -1)
    sides = [
        jnp.concatenate(list(cols), 1).reshape(3, rows_mid, WT, 3 * HD)
        for cols in ((left, hidden, hidden), (hidden, hidden, right))
    ]
    out_rows = 2 * band_rows
    acc = jnp.zeros((2 * out_rows * WT, HD), F32)
    for i in range(3):
        for j in range(3):
            window = jnp.concatenate(
                [side[i, (y + j + 1) // 2] for side in sides for y in range(out_rows)], 0
            ).astype(BF16)
            acc += jnp.dot(window, conv2[i * 3 + j], preferred_element_type=F32)
    acc = acc + bias2_ref[...]
    for p in range(2):
        for y in range(out_rows):
            first = (p * out_rows + y) * WT
            outf[y, pl.ds(p, WT, 2), :] = acc[first : first + WT]
    out_ref[0] = outf[...].astype(BF16)

    for copy in pending:
        copy.wait_send()

    def sent(i, carry):
        pltpu.make_async_remote_copy(
            src_ref=part.at[lax.rem(me + i, group_n)],
            dst_ref=rsbuf.at[me],
            send_sem=rs_send.at[i],
            recv_sem=rs_recv.at[i],
            device_id={"frames": f, "bands": b},
            device_id_type=MESH,
        ).wait_send()
        return carry

    lax.fori_loop(1, group_n, sent, 0, unroll=group_n <= 16)
    for age, e in offsets:

        @pl.when(sends(age, e))
        def _(age=age, e=e):
            hand(age, e).wait_send()


def local(
    frames_n,
    bands_n,
    span_tokens,
    w_query,
    w_key,
    w_value,
    cache_keys,
    cache_values,
    frame_counts,
    rollback_start,
    w_proj,
    norm_gain,
    conv_first,
    bias_first,
    conv_second,
    bias_second,
):
    _, slot_n, width = span_tokens.shape
    cached_n, _, lw = cache_keys.shape
    rows = cached_n * slot_n
    cw = 256 if lw % 256 == 0 else 128
    chunk_n = lw // cw
    heads = lw // HD
    q_total = frames_n * slot_n
    part_rows = slot_n // bands_n
    band_rows = part_rows // WT
    reach = 2 // band_rows
    key_rows = rows + HD
    group_n = frames_n * bands_n
    anywhere = pl.BlockSpec(memory_space=pl.ANY)
    smem = pl.BlockSpec(memory_space=pltpu.SMEM)
    vmem = pl.BlockSpec(memory_space=pltpu.VMEM)
    dma = pltpu.SemaphoreType.DMA
    return pl.pallas_call(
        functools.partial(kernel, frames_n, bands_n),
        out_shape=pltpu.VMEM((1, 2 * band_rows, 2 * WT, HD), BF16),
        in_specs=[smem, smem] + [anywhere] * 7 + [vmem, anywhere, vmem, anywhere, vmem],
        out_specs=vmem,
        scratch_shapes=[
            pltpu.VMEM((slot_n, width), BF16),
            pltpu.VMEM((chunk_n, width, cw), BF16),
            pltpu.VMEM((chunk_n, width, cw), BF16),
            pltpu.VMEM((chunk_n, width, cw), BF16),
            pltpu.VMEM((key_rows, lw), BF16),
            pltpu.VMEM((key_rows, lw), BF16),
            pltpu.VMEM((lw, HD), BF16),
            pltpu.VMEM((9, 3 * HD, HD), BF16),
            pltpu.VMEM((9, 3 * HD, HD), BF16),
            pltpu.VMEM((chunk_n, frames_n, slot_n, cw), BF16),
            pltpu.VMEM((heads, q_total, key_rows), BF16),
            pltpu.VMEM((heads, q_total, HD), F32),
            pltpu.VMEM((frames_n, 16, q_total), F32),
            pltpu.VMEM((group_n, part_rows, HD), BF16),
            pltpu.VMEM((group_n, part_rows, HD), BF16),
            pltpu.VMEM((AGES, 2 * reach + 1, part_rows, HD), BF16),
            pltpu.VMEM((2 * band_rows, 2 * WT, HD), F32),
            dma((6 + 3 * chunk_n,)),
            dma((chunk_n, frames_n)),
            dma((chunk_n, frames_n)),
            dma((chunk_n, frames_n)),
            dma((chunk_n, frames_n)),
            pltpu.SemaphoreType.REGULAR((2,)),
            dma((frames_n,)),
            dma((frames_n,)),
            dma((group_n,)),
            dma((group_n,)),
            dma((AGES, 2 * reach + 1)),
            dma((AGES, 2 * reach + 1)),
        ],
        compiler_params=pltpu.CompilerParams(
            collective_id=0, has_side_effects=True, vmem_limit_bytes=60 * 1024 * 1024
        ),
    )(
        frame_counts,
        rollback_start,
        span_tokens.reshape(slot_n, width),
        w_query,
        w_key,
        w_value,
        cache_keys.reshape(rows, lw),
        cache_values.reshape(rows, lw),
        w_proj,
        norm_gain.reshape(1, HD),
        conv_first.reshape(9, 3 * HD, HD),
        bias_first.reshape(1, HD),
        conv_second.reshape(9, 3 * HD, HD),
        bias_second.reshape(1, HD),
    )


def solution(mesh):
    placed = (
        P(("groups", "frames"), None, None),
        P(None, "bands"),
        P(None, "bands"),
        P(None, "bands"),
        P(("groups", "frames"), None, "bands"),
        P(("groups", "frames"), None, "bands"),
        P(("groups", "frames")),
        P("groups"),
        P("bands", None),
        P(),
        P(),
        P(),
        P(),
        P(),
    )
    return jax.shard_map(
        functools.partial(local, mesh.shape["frames"], mesh.shape["bands"]),
        mesh=mesh,
        in_specs=placed,
        out_specs=P(("groups", "frames"), "bands", None, None),
        check_vma=False,
    )
```

```python
import functools
import math

import jax
import jax.numpy as jnp
from jax import lax
from jax.experimental import pallas as pl
from jax.experimental.pallas import tpu as pltpu
from jax.sharding import PartitionSpec as P

HD = 128
WT = 8
AGES = 5
MESH = pl.DeviceIdType.MESH
F32 = jnp.float32
BF16 = jnp.bfloat16
NEG = -1e30


def rolled(x, steps):
    rows = x.shape[0]
    column = lax.broadcasted_iota(jnp.int32, x.shape, 0) % WT
    edge = 0 if steps == 1 else WT - 1
    return jnp.where(column == edge, 0.0, pltpu.roll(x, steps % rows, 0))


def kernel(
    frames_n,
    bands_n,
    counts_ref,
    start_ref,
    tokens_hbm,
    wq_hbm,
    wk_hbm,
    wv_hbm,
    keys_hbm,
    values_hbm,
    proj_hbm,
    gain_ref,
    conv1_hbm,
    bias1_ref,
    conv2_hbm,
    bias2_ref,
    out_ref,
    tok,
    wq,
    wk,
    wv,
    kbuf,
    vbuf,
    proj,
    conv1,
    conv2,
    qall,
    pbuf,
    obuf,
    stats,
    part,
    rsbuf,
    lat,
    outf,
    in_sem,
    q_send,
    q_recv,
    pass_send,
    pass_recv,
    chain,
    st_send,
    st_recv,
    rs_send,
    rs_recv,
    ag_send,
    ag_recv,
):
    f = lax.axis_index("frames")
    b = lax.axis_index("bands")
    group_n = frames_n * bands_n
    me = f * bands_n + b
    slot_n = tok.shape[0]
    chunk_n, _, cw = wq.shape
    cached_n = counts_ref.shape[0]
    cached_rows = cached_n * slot_n
    heads = chunk_n * cw // HD
    q_total = frames_n * slot_n
    part_rows = slot_n // bands_n
    band_rows = part_rows // WT
    reach = 2 // band_rows

    sem_i = [0]
    loads = {}

    def load(name, src, dst):
        copy = pltpu.make_async_copy(src, dst, in_sem.at[sem_i[0]])
        sem_i[0] += 1
        copy.start()
        loads[name] = copy

    load("tok", tokens_hbm, tok)
    for c in range(chunk_n):
        load(("q", c), wq_hbm.at[:, pl.ds(c * cw, cw)], wq.at[c])
    for c in range(chunk_n):
        load(("k", c), wk_hbm.at[:, pl.ds(c * cw, cw)], wk.at[c])
    for c in range(chunk_n):
        load(("v", c), wv_hbm.at[:, pl.ds(c * cw, cw)], wv.at[c])
    load("keys", keys_hbm, kbuf.at[pl.ds(0, cached_rows)])
    load("values", values_hbm, vbuf.at[pl.ds(0, cached_rows)])
    load("proj", proj_hbm, proj)
    load("conv1", conv1_hbm, conv1)
    load("conv2", conv2_hbm, conv2)

    lat[...] = jnp.zeros_like(lat)
    barrier = pltpu.get_barrier_semaphore()

    def greet(i, carry):
        pl.semaphore_signal(
            barrier,
            inc=1,
            device_id={"frames": lax.rem(f + i, frames_n)},
            device_id_type=MESH,
        )
        return carry

    lax.fori_loop(1, frames_n, greet, 0)

    def beside(sem, step):
        pl.semaphore_signal(sem, inc=1, device_id={"bands": b + step}, device_id_type=MESH)

    @pl.when(b > 0)
    def _():
        beside(barrier, -1)

    @pl.when(b < bands_n - 1)
    def _():
        beside(barrier, 1)

    greeted = frames_n - 1 + (b > 0).astype(jnp.int32) + (b < bands_n - 1).astype(jnp.int32)

    def relay_entry(step):
        if step > 0:

            @pl.when(b == step)
            def _():
                pl.semaphore_wait(chain.at[0], 1)

            @pl.when(b == bands_n - 1 - step)
            def _():
                pl.semaphore_wait(chain.at[1], 1)

        if step < bands_n - 1:

            @pl.when(b == step)
            def _():
                beside(chain.at[0], 1)

            @pl.when(b == bands_n - 1 - step)
            def _():
                beside(chain.at[1], -1)

    pad_rows = kbuf.shape[0] - cached_rows - slot_n
    kbuf[pl.ds(cached_rows + slot_n, pad_rows), :] = jnp.zeros((pad_rows, kbuf.shape[1]), BF16)
    vbuf[pl.ds(cached_rows + slot_n, pad_rows), :] = jnp.zeros((pad_rows, kbuf.shape[1]), BF16)

    pending = []

    def remote(src, dst, send, recv, target, begin=True):
        copy = pltpu.make_async_remote_copy(
            src_ref=src,
            dst_ref=dst,
            send_sem=send,
            recv_sem=recv,
            device_id={"frames": target},
            device_id_type=MESH,
        )
        if begin:
            copy.start()
            pending.append(copy)
        return copy

    share = 2 if frames_n % 2 == 0 else 1
    core = lax.rem(f, share)
    node = f // share
    nodes = frames_n // share
    mate = f + 1 - 2 * core if share == 2 else f
    first = 0 if share == 2 else 1

    def query_copy(c, d, begin):
        step = d if begin else nodes - d
        target = lax.rem(node + step, nodes) * share + core if d > 0 else mate
        rows = qall.at[c, f if begin else target]
        return remote(rows, rows, q_send.at[c, d], q_recv.at[c, d], target, begin)

    def pass_copy(c, d, begin):
        source = lax.rem(node + nodes - d, nodes) * share
        rows = qall.at[c, source + (core if begin else 1 - core)]
        return remote(rows, rows, pass_send.at[c, d], pass_recv.at[c, d], mate, begin)

    def relay_queries(c):
        for d in range(1, nodes):
            query_copy(c, d, False).wait_recv()
            if share == 2:
                pass_copy(c, d, True)

    loads["tok"].wait()
    scale = HD ** (-0.5) * math.log2(math.e)
    for c in range(chunk_n):
        loads[("q", c)].wait()
        queries = jnp.dot(tok[...], wq[c], preferred_element_type=F32) * scale
        qall[c, f] = queries.astype(BF16)
        if c == 0:
            pl.semaphore_wait(barrier, greeted)
        for d in [*range(1, nodes), *range(first, 1)]:
            query_copy(c, d, True)
    relay_entry(0)
    for c in range(chunk_n):
        loads[("k", c)].wait()
        kbuf[pl.ds(cached_rows, slot_n), pl.ds(c * cw, cw)] = jnp.dot(
            tok[...], wk[c], preferred_element_type=F32
        ).astype(BF16)
    for c in range(chunk_n):
        loads[("v", c)].wait()
        vbuf[pl.ds(cached_rows, slot_n), pl.ds(c * cw, cw)] = jnp.dot(
            tok[...], wv[c], preferred_element_type=F32
        ).astype(BF16)
        relay_queries(c)
    if bands_n > 1:
        relay_entry(1)

    lane = lax.broadcasted_iota(jnp.int32, (1, HD), 1)
    per_tile = HD // slot_n
    bias_tiles = []
    for tile in range(cached_rows // HD):
        visible = lane < 0
        for s in range(per_tile):
            g = tile * per_tile + s
            slot = lane - s * slot_n
            shown = (slot >= 0) & (slot < counts_ref[g]) & (slot < slot_n)
            visible = visible | (shown & ((lane * 0 + (f * cached_n + g)) < start_ref[0]))
        bias_tiles.append(jnp.where(visible, 0.0, NEG))
    bias_row = jnp.concatenate(bias_tiles, 1)

    q_block = min(q_total, 256)
    row = lax.broadcasted_iota(jnp.int32, (q_block, HD), 0)
    wide_lane = lax.broadcasted_iota(jnp.int32, (q_block, HD), 1)

    loads["keys"].wait()
    loads["values"].wait()

    def settle(c):
        if share == 2:
            query_copy(c, 0, False).wait_recv()
            for d in range(1, nodes):
                pass_copy(c, d, False).wait_recv()

    def weigh(h, block):
        per = q_block // slot_n
        q = qall[h * HD // cw, pl.ds(block * per, per), :, pl.ds(h * HD % cw, HD)]
        q = q.reshape(q_block, HD)
        k = kbuf[:, pl.ds(h * HD, HD)]
        raw = lax.dot_general(q, k, (((1,), (1,)), ((), ())), preferred_element_type=F32)
        old = raw[:, :cached_rows] + bias_row
        new = jnp.where(
            (wide_lane < slot_n) & (row + block * q_block >= f * slot_n),
            raw[:, cached_rows:],
            NEG,
        )
        top = jnp.maximum(jnp.max(old, 1, keepdims=True), jnp.max(new, 1, keepdims=True))
        w_old = jnp.exp2(old - top)
        w_new = jnp.exp2(new - top)
        total = jnp.sum(w_old, 1, keepdims=True) + jnp.sum(w_new, 1, keepdims=True)
        pbuf[h, pl.ds(block * q_block, q_block), pl.ds(0, cached_rows)] = w_old.astype(BF16)
        pbuf[h, pl.ds(block * q_block, q_block), pl.ds(cached_rows, HD)] = w_new.astype(BF16)
        return top, total

    def gather(h, block):
        rows = pl.ds(block * q_block, q_block)
        obuf[h, rows, :] = jnp.dot(
            pbuf[h, rows, :], vbuf[:, pl.ds(h * HD, HD)], preferred_element_type=F32
        )

    blocks = range(q_total // q_block)
    late = heads
    for block in blocks:
        stat = jnp.zeros((q_block, HD), F32)
        for h in range(heads):
            if block == 0 and h * HD % cw == 0:
                settle(h * HD // cw)
            top, total = weigh(h, block)
            stat = jnp.where(wide_lane == h, top, stat)
            stat = jnp.where(wide_lane == 8 + h, total, stat)
            if h < heads - late:
                gather(h, block)
        stats[f, :, pl.ds(block * q_block, q_block)] = jnp.transpose(stat)[:16]
    if bands_n > 2:
        relay_entry(2)
    for d in range(1, frames_n):
        copy = pltpu.make_async_remote_copy(
            src_ref=stats.at[f],
            dst_ref=stats.at[f],
            send_sem=st_send.at[d],
            recv_sem=st_recv.at[d],
            device_id={"frames": lax.rem(f + d, frames_n)},
            device_id_type=MESH,
        )
        copy.start()
        pending.append(copy)
    for block in blocks:
        for h in range(heads - late, heads):
            gather(h, block)
    for d in range(1, frames_n):
        source = lax.rem(f + frames_n - d, frames_n)
        pltpu.make_async_remote_copy(
            src_ref=stats.at[source],
            dst_ref=stats.at[source],
            send_sem=st_send.at[d],
            recv_sem=st_recv.at[d],
            device_id={"frames": source},
            device_id_type=MESH,
        ).wait_recv()
    for step in range(3, bands_n):
        relay_entry(step)
    loads["proj"].wait()
    top = stats[0, :8]
    for k in range(1, frames_n):
        top = jnp.maximum(top, stats[k, :8])
    summed = jnp.zeros_like(top)
    for k in range(frames_n):
        summed += jnp.exp2(stats[k, :8] - top) * stats[k, 8:16]
    head_row = lax.broadcasted_iota(jnp.int32, top.shape, 0)
    factor = jnp.where(head_row < heads, jnp.exp2(stats[f, :8] - top) / summed, 0.0)
    factor = jnp.concatenate([factor, jnp.zeros((HD - 8, q_total), F32)], 0)
    for block in blocks:
        rows = pl.ds(block * q_block, q_block)
        column = jnp.transpose(factor[:, block * q_block : (block + 1) * q_block])
        scaled = jnp.concatenate(
            [(obuf[h, rows, :] * column[:, h : h + 1]).astype(BF16) for h in range(heads)], 1
        )
        partial = jnp.dot(scaled, proj[...], preferred_element_type=F32).astype(BF16)
        per = q_block // part_rows
        part[pl.ds(block * per, per)] = partial.reshape(per, part_rows, HD)

    def scatter(i, carry):
        other = lax.rem(me + i, group_n)
        pltpu.make_async_remote_copy(
            src_ref=part.at[other],
            dst_ref=rsbuf.at[me],
            send_sem=rs_send.at[i],
            recv_sem=rs_recv.at[i],
            device_id={"frames": other // bands_n, "bands": lax.rem(other, bands_n)},
            device_id_type=MESH,
        ).start()
        return carry

    lax.fori_loop(1, group_n, scatter, 0, unroll=group_n <= 16)
    rsbuf[me] = part[me]
    loads["conv1"].wait()
    loads["conv2"].wait()

    def received(i, carry):
        other = lax.rem(me + group_n - i, group_n)
        copy = pltpu.make_async_remote_copy(
            src_ref=part.at[other],
            dst_ref=rsbuf.at[other],
            send_sem=rs_send.at[i],
            recv_sem=rs_recv.at[i],
            device_id={"frames": other // bands_n, "bands": lax.rem(other, bands_n)},
            device_id_type=MESH,
        )
        copy.wait_recv()
        return carry

    lax.fori_loop(1, group_n, received, 0, unroll=group_n <= 16)
    own = jnp.sum(rsbuf[...].astype(F32), 0)
    lat[AGES - 1, reach] = own.astype(BF16)

    offsets = [
        (age, e)
        for age in range(min(AGES, frames_n))
        for e in range(-reach, reach + 1)
        if (age, e) != (0, 0)
    ]

    def hand(age, e):
        return pltpu.make_async_remote_copy(
            src_ref=lat.at[AGES - 1, reach],
            dst_ref=lat.at[AGES - 1 - age, reach - e],
            send_sem=ag_send.at[age, e + reach],
            recv_sem=ag_recv.at[age, e + reach],
            device_id={
                "frames": lax.rem(f + age, frames_n),
                "bands": lax.rem(b + e + bands_n, bands_n),
            },
            device_id_type=MESH,
        )

    def sends(age, e):
        return (f + age < frames_n) & (b + e >= 0) & (b + e < bands_n)

    def takes(age, e):
        return (f - age >= 0) & (b - e >= 0) & (b - e < bands_n)

    for age, e in offsets:

        @pl.when(sends(age, e))
        def _(age=age, e=e):
            hand(age, e).start()

    for age, e in offsets:

        @pl.when(takes(age, e))
        def _(age=age, e=e):
            hand(age, e).wait_recv()

    rows_in = band_rows + 4
    rows_mid = band_rows + 2
    latent = lat[...].astype(F32).reshape(AGES, rows_in, WT, HD)
    flat = latent.reshape(AGES * rows_in * WT, HD)
    mean_square = jnp.mean(flat * flat, -1, keepdims=True)
    normed = flat * lax.rsqrt(mean_square + 1e-06) * gain_ref[...]
    active = (normed * jax.nn.sigmoid(normed)).astype(BF16).astype(F32)
    taps = jnp.concatenate([rolled(active, 1), active, rolled(active, -1)], 1)
    taps = taps.reshape(AGES, rows_in, WT, 3 * HD)
    mid = 3 * rows_mid * WT
    acc = jnp.zeros((mid, HD), F32)
    for i in range(3):
        for j in range(3):
            window = taps[i : i + 3, j : j + rows_mid].reshape(mid, 3 * HD).astype(BF16)
            acc += jnp.dot(window, conv1[i * 3 + j], preferred_element_type=F32)
    centre = latent[2:, 1 : 1 + rows_mid].reshape(mid, HD)
    index = lax.broadcasted_iota(jnp.int32, (mid, HD), 0)
    at_frame = index // (rows_mid * WT) + f - 2
    at_row = index // WT % rows_mid + b * band_rows - 1
    inside = (at_frame >= 0) & (at_row >= 0) & (at_row < bands_n * band_rows)
    hidden = jnp.where(inside, centre + (acc + bias1_ref[...]), 0.0).astype(BF16).astype(F32)
    left, right = rolled(hidden, 1), rolled(hidden, -1)
    sides = [
        jnp.concatenate(list(cols), 1).reshape(3, rows_mid, WT, 3 * HD)
        for cols in ((left, hidden, hidden), (hidden, hidden, right))
    ]
    out_rows = 2 * band_rows
    acc = jnp.zeros((2 * out_rows * WT, HD), F32)
    for i in range(3):
        for j in range(3):
            window = jnp.concatenate(
                [side[i, (y + j + 1) // 2] for side in sides for y in range(out_rows)], 0
            ).astype(BF16)
            acc += jnp.dot(window, conv2[i * 3 + j], preferred_element_type=F32)
    acc = acc + bias2_ref[...]
    for p in range(2):
        for y in range(out_rows):
            first = (p * out_rows + y) * WT
            outf[y, pl.ds(p, WT, 2), :] = acc[first : first + WT]
    out_ref[0] = outf[...].astype(BF16)

    for copy in pending:
        copy.wait_send()

    def sent(i, carry):
        pltpu.make_async_remote_copy(
            src_ref=part.at[lax.rem(me + i, group_n)],
            dst_ref=rsbuf.at[me],
            send_sem=rs_send.at[i],
            recv_sem=rs_recv.at[i],
            device_id={"frames": f, "bands": b},
            device_id_type=MESH,
        ).wait_send()
        return carry

    lax.fori_loop(1, group_n, sent, 0, unroll=group_n <= 16)
    for age, e in offsets:

        @pl.when(sends(age, e))
        def _(age=age, e=e):
            hand(age, e).wait_send()


def local(
    frames_n,
    bands_n,
    span_tokens,
    w_query,
    w_key,
    w_value,
    cache_keys,
    cache_values,
    frame_counts,
    rollback_start,
    w_proj,
    norm_gain,
    conv_first,
    bias_first,
    conv_second,
    bias_second,
):
    _, slot_n, width = span_tokens.shape
    cached_n, _, lw = cache_keys.shape
    rows = cached_n * slot_n
    cw = 256 if lw % 256 == 0 else 128
    chunk_n = lw // cw
    heads = lw // HD
    q_total = frames_n * slot_n
    part_rows = slot_n // bands_n
    band_rows = part_rows // WT
    reach = 2 // band_rows
    key_rows = rows + HD
    group_n = frames_n * bands_n
    anywhere = pl.BlockSpec(memory_space=pl.ANY)
    smem = pl.BlockSpec(memory_space=pltpu.SMEM)
    vmem = pl.BlockSpec(memory_space=pltpu.VMEM)
    dma = pltpu.SemaphoreType.DMA
    return pl.pallas_call(
        functools.partial(kernel, frames_n, bands_n),
        out_shape=pltpu.VMEM((1, 2 * band_rows, 2 * WT, HD), BF16),
        in_specs=[smem, smem] + [anywhere] * 7 + [vmem, anywhere, vmem, anywhere, vmem],
        out_specs=vmem,
        scratch_shapes=[
            pltpu.VMEM((slot_n, width), BF16),
            pltpu.VMEM((chunk_n, width, cw), BF16),
            pltpu.VMEM((chunk_n, width, cw), BF16),
            pltpu.VMEM((chunk_n, width, cw), BF16),
            pltpu.VMEM((key_rows, lw), BF16),
            pltpu.VMEM((key_rows, lw), BF16),
            pltpu.VMEM((lw, HD), BF16),
            pltpu.VMEM((9, 3 * HD, HD), BF16),
            pltpu.VMEM((9, 3 * HD, HD), BF16),
            pltpu.VMEM((chunk_n, frames_n, slot_n, cw), BF16),
            pltpu.VMEM((heads, q_total, key_rows), BF16),
            pltpu.VMEM((heads, q_total, HD), F32),
            pltpu.VMEM((frames_n, 16, q_total), F32),
            pltpu.VMEM((group_n, part_rows, HD), BF16),
            pltpu.VMEM((group_n, part_rows, HD), BF16),
            pltpu.VMEM((AGES, 2 * reach + 1, part_rows, HD), BF16),
            pltpu.VMEM((2 * band_rows, 2 * WT, HD), F32),
            dma((6 + 3 * chunk_n,)),
            dma((chunk_n, frames_n)),
            dma((chunk_n, frames_n)),
            dma((chunk_n, frames_n)),
            dma((chunk_n, frames_n)),
            pltpu.SemaphoreType.REGULAR((2,)),
            dma((frames_n,)),
            dma((frames_n,)),
            dma((group_n,)),
            dma((group_n,)),
            dma((AGES, 2 * reach + 1)),
            dma((AGES, 2 * reach + 1)),
        ],
        compiler_params=pltpu.CompilerParams(
            collective_id=0, has_side_effects=True, vmem_limit_bytes=60 * 1024 * 1024
        ),
    )(
        frame_counts,
        rollback_start,
        span_tokens.reshape(slot_n, width),
        w_query,
        w_key,
        w_value,
        cache_keys.reshape(rows, lw),
        cache_values.reshape(rows, lw),
        w_proj,
        norm_gain.reshape(1, HD),
        conv_first.reshape(9, 3 * HD, HD),
        bias_first.reshape(1, HD),
        conv_second.reshape(9, 3 * HD, HD),
        bias_second.reshape(1, HD),
    )


def solution(mesh):
    placed = (
        P(("groups", "frames"), None, None),
        P(None, "bands"),
        P(None, "bands"),
        P(None, "bands"),
        P(("groups", "frames"), None, "bands"),
        P(("groups", "frames"), None, "bands"),
        P(("groups", "frames")),
        P("groups"),
        P("bands", None),
        P(),
        P(),
        P(),
        P(),
        P(),
    )
    return jax.shard_map(
        functools.partial(local, mesh.shape["frames"], mesh.shape["bands"]),
        mesh=mesh,
        in_specs=placed,
        out_specs=P(("groups", "frames"), "bands", None, None),
        check_vma=False,
    )
```

```python
import functools
import math

import jax
import jax.numpy as jnp
from jax import lax
from jax.experimental import pallas as pl
from jax.experimental.pallas import tpu as pltpu
from jax.sharding import PartitionSpec as P

HD = 128
WT = 8
AGES = 5
MESH = pl.DeviceIdType.MESH
F32 = jnp.float32
BF16 = jnp.bfloat16
NEG = -1e30


def rolled(x, steps):
    rows = x.shape[0]
    column = lax.broadcasted_iota(jnp.int32, x.shape, 0) % WT
    edge = 0 if steps == 1 else WT - 1
    return jnp.where(column == edge, 0.0, pltpu.roll(x, steps % rows, 0))


def kernel(
    frames_n,
    bands_n,
    counts_ref,
    start_ref,
    tokens_hbm,
    wq_hbm,
    wk_hbm,
    wv_hbm,
    keys_hbm,
    values_hbm,
    proj_hbm,
    gain_ref,
    conv1_hbm,
    bias1_ref,
    conv2_hbm,
    bias2_ref,
    out_ref,
    tok,
    wq,
    wk,
    wv,
    kbuf,
    vbuf,
    proj,
    conv1,
    conv2,
    qall,
    pbuf,
    obuf,
    stats,
    part,
    rsbuf,
    lat,
    outf,
    in_sem,
    q_send,
    q_recv,
    pass_send,
    pass_recv,
    chain,
    st_send,
    st_recv,
    rs_send,
    rs_recv,
    ag_send,
    ag_recv,
):
    f = lax.axis_index("frames")
    b = lax.axis_index("bands")
    group_n = frames_n * bands_n
    me = f * bands_n + b
    slot_n = tok.shape[0]
    chunk_n, _, cw = wq.shape
    cached_n = counts_ref.shape[0]
    cached_rows = cached_n * slot_n
    heads = chunk_n * cw // HD
    q_total = frames_n * slot_n
    part_rows = slot_n // bands_n
    band_rows = part_rows // WT
    reach = 2 // band_rows

    sem_i = [0]
    loads = {}

    def load(name, src, dst):
        copy = pltpu.make_async_copy(src, dst, in_sem.at[sem_i[0]])
        sem_i[0] += 1
        copy.start()
        loads[name] = copy

    load("tok", tokens_hbm, tok)
    for c in range(chunk_n):
        load(("q", c), wq_hbm.at[:, pl.ds(c * cw, cw)], wq.at[c])
    for c in range(chunk_n):
        load(("k", c), wk_hbm.at[:, pl.ds(c * cw, cw)], wk.at[c])
    load("keys", keys_hbm, kbuf.at[pl.ds(0, cached_rows)])
    for c in range(chunk_n):
        load(("v", c), wv_hbm.at[:, pl.ds(c * cw, cw)], wv.at[c])
    load("values", values_hbm, vbuf.at[pl.ds(0, cached_rows)])
    load("proj", proj_hbm, proj)
    load("conv1", conv1_hbm, conv1)
    load("conv2", conv2_hbm, conv2)

    lat[...] = jnp.zeros_like(lat)
    barrier = pltpu.get_barrier_semaphore()

    def greet(i, carry):
        pl.semaphore_signal(
            barrier,
            inc=1,
            device_id={"frames": lax.rem(f + i, frames_n)},
            device_id_type=MESH,
        )
        return carry

    lax.fori_loop(1, frames_n, greet, 0)

    def beside(sem, step):
        pl.semaphore_signal(sem, inc=1, device_id={"bands": b + step}, device_id_type=MESH)

    @pl.when(b > 0)
    def _():
        beside(barrier, -1)

    @pl.when(b < bands_n - 1)
    def _():
        beside(barrier, 1)

    greeted = frames_n - 1 + (b > 0).astype(jnp.int32) + (b < bands_n - 1).astype(jnp.int32)

    def relay_entry(step):
        if step > 0:

            @pl.when(b == step)
            def _():
                pl.semaphore_wait(chain.at[0], 1)

            @pl.when(b == bands_n - 1 - step)
            def _():
                pl.semaphore_wait(chain.at[1], 1)

        if step < bands_n - 1:

            @pl.when(b == step)
            def _():
                beside(chain.at[0], 1)

            @pl.when(b == bands_n - 1 - step)
            def _():
                beside(chain.at[1], -1)

    pad_rows = kbuf.shape[0] - cached_rows - slot_n
    kbuf[pl.ds(cached_rows + slot_n, pad_rows), :] = jnp.zeros((pad_rows, kbuf.shape[1]), BF16)
    vbuf[pl.ds(cached_rows + slot_n, pad_rows), :] = jnp.zeros((pad_rows, kbuf.shape[1]), BF16)

    pending = []

    def remote(src, dst, send, recv, target, begin=True):
        copy = pltpu.make_async_remote_copy(
            src_ref=src,
            dst_ref=dst,
            send_sem=send,
            recv_sem=recv,
            device_id={"frames": target},
            device_id_type=MESH,
        )
        if begin:
            copy.start()
            pending.append(copy)
        return copy

    share = 2 if frames_n % 2 == 0 else 1
    core = lax.rem(f, share)
    node = f // share
    nodes = frames_n // share
    mate = f + 1 - 2 * core if share == 2 else f
    first = 0 if share == 2 else 1

    def query_copy(c, d, begin):
        step = d if begin else nodes - d
        target = lax.rem(node + step, nodes) * share + core if d > 0 else mate
        rows = qall.at[c, f if begin else target]
        return remote(rows, rows, q_send.at[c, d], q_recv.at[c, d], target, begin)

    def pass_copy(c, d, begin):
        source = lax.rem(node + nodes - d, nodes) * share
        rows = qall.at[c, source + (core if begin else 1 - core)]
        return remote(rows, rows, pass_send.at[c, d], pass_recv.at[c, d], mate, begin)

    def relay_queries(c):
        for d in range(1, nodes):
            query_copy(c, d, False).wait_recv()
            if share == 2:
                pass_copy(c, d, True)

    loads["tok"].wait()
    scale = HD ** (-0.5) * math.log2(math.e)
    for c in range(chunk_n):
        loads[("q", c)].wait()
        queries = jnp.dot(tok[...], wq[c], preferred_element_type=F32) * scale
        qall[c, f] = queries.astype(BF16)
        if c == 0:
            pl.semaphore_wait(barrier, greeted)
        for d in [*range(1, nodes), *range(first, 1)]:
            query_copy(c, d, True)
    relay_entry(0)
    for c in range(chunk_n):
        loads[("k", c)].wait()
        kbuf[pl.ds(cached_rows, slot_n), pl.ds(c * cw, cw)] = jnp.dot(
            tok[...], wk[c], preferred_element_type=F32
        ).astype(BF16)
    for c in range(chunk_n):
        relay_queries(c)
    if bands_n > 1:
        relay_entry(1)

    lane = lax.broadcasted_iota(jnp.int32, (1, HD), 1)
    per_tile = HD // slot_n
    bias_tiles = []
    for tile in range(cached_rows // HD):
        visible = lane < 0
        for s in range(per_tile):
            g = tile * per_tile + s
            slot = lane - s * slot_n
            shown = (slot >= 0) & (slot < counts_ref[g]) & (slot < slot_n)
            visible = visible | (shown & ((lane * 0 + (f * cached_n + g)) < start_ref[0]))
        bias_tiles.append(jnp.where(visible, 0.0, NEG))
    bias_row = jnp.concatenate(bias_tiles, 1)

    q_block = min(q_total, 256)
    row = lax.broadcasted_iota(jnp.int32, (q_block, HD), 0)
    wide_lane = lax.broadcasted_iota(jnp.int32, (q_block, HD), 1)

    loads["keys"].wait()

    def settle(c):
        if share == 2:
            query_copy(c, 0, False).wait_recv()
            for d in range(1, nodes):
                pass_copy(c, d, False).wait_recv()

    def weigh(h, block):
        per = q_block // slot_n
        q = qall[h * HD // cw, pl.ds(block * per, per), :, pl.ds(h * HD % cw, HD)]
        q = q.reshape(q_block, HD)
        k = kbuf[:, pl.ds(h * HD, HD)]
        raw = lax.dot_general(q, k, (((1,), (1,)), ((), ())), preferred_element_type=F32)
        old = raw[:, :cached_rows] + bias_row
        new = jnp.where(
            (wide_lane < slot_n) & (row + block * q_block >= f * slot_n),
            raw[:, cached_rows:],
            NEG,
        )
        top = jnp.maximum(jnp.max(old, 1, keepdims=True), jnp.max(new, 1, keepdims=True))
        w_old = jnp.exp2(old - top)
        w_new = jnp.exp2(new - top)
        total = jnp.sum(w_old, 1, keepdims=True) + jnp.sum(w_new, 1, keepdims=True)
        pbuf[h, pl.ds(block * q_block, q_block), pl.ds(0, cached_rows)] = w_old.astype(BF16)
        pbuf[h, pl.ds(block * q_block, q_block), pl.ds(cached_rows, HD)] = w_new.astype(BF16)
        return top, total

    def gather(h, block):
        rows = pl.ds(block * q_block, q_block)
        obuf[h, rows, :] = jnp.dot(
            pbuf[h, rows, :], vbuf[:, pl.ds(h * HD, HD)], preferred_element_type=F32
        )

    blocks = range(q_total // q_block)
    late = heads
    for block in blocks:
        stat = jnp.zeros((q_block, HD), F32)
        for h in range(heads):
            if block == 0 and h * HD % cw == 0:
                settle(h * HD // cw)
            top, total = weigh(h, block)
            stat = jnp.where(wide_lane == h, top, stat)
            stat = jnp.where(wide_lane == 8 + h, total, stat)
            if h < heads - late:
                gather(h, block)
        stats[f, :, pl.ds(block * q_block, q_block)] = jnp.transpose(stat)[:16]
    if bands_n > 2:
        relay_entry(2)
    for d in range(1, frames_n):
        copy = pltpu.make_async_remote_copy(
            src_ref=stats.at[f],
            dst_ref=stats.at[f],
            send_sem=st_send.at[d],
            recv_sem=st_recv.at[d],
            device_id={"frames": lax.rem(f + d, frames_n)},
            device_id_type=MESH,
        )
        copy.start()
        pending.append(copy)
    for c in range(chunk_n):
        loads[("v", c)].wait()
        vbuf[pl.ds(cached_rows, slot_n), pl.ds(c * cw, cw)] = jnp.dot(
            tok[...], wv[c], preferred_element_type=F32
        ).astype(BF16)
    loads["values"].wait()
    for block in blocks:
        for h in range(heads - late, heads):
            gather(h, block)
    for d in range(1, frames_n):
        source = lax.rem(f + frames_n - d, frames_n)
        pltpu.make_async_remote_copy(
            src_ref=stats.at[source],
            dst_ref=stats.at[source],
            send_sem=st_send.at[d],
            recv_sem=st_recv.at[d],
            device_id={"frames": source},
            device_id_type=MESH,
        ).wait_recv()
    for step in range(3, bands_n):
        relay_entry(step)
    loads["proj"].wait()
    top = stats[0, :8]
    for k in range(1, frames_n):
        top = jnp.maximum(top, stats[k, :8])
    summed = jnp.zeros_like(top)
    for k in range(frames_n):
        summed += jnp.exp2(stats[k, :8] - top) * stats[k, 8:16]
    head_row = lax.broadcasted_iota(jnp.int32, top.shape, 0)
    factor = jnp.where(head_row < heads, jnp.exp2(stats[f, :8] - top) / summed, 0.0)
    factor = jnp.concatenate([factor, jnp.zeros((HD - 8, q_total), F32)], 0)
    for block in blocks:
        rows = pl.ds(block * q_block, q_block)
        column = jnp.transpose(factor[:, block * q_block : (block + 1) * q_block])
        scaled = jnp.concatenate(
            [(obuf[h, rows, :] * column[:, h : h + 1]).astype(BF16) for h in range(heads)], 1
        )
        partial = jnp.dot(scaled, proj[...], preferred_element_type=F32).astype(BF16)
        per = q_block // part_rows
        part[pl.ds(block * per, per)] = partial.reshape(per, part_rows, HD)

    def scatter(i, carry):
        other = lax.rem(me + i, group_n)
        pltpu.make_async_remote_copy(
            src_ref=part.at[other],
            dst_ref=rsbuf.at[me],
            send_sem=rs_send.at[i],
            recv_sem=rs_recv.at[i],
            device_id={"frames": other // bands_n, "bands": lax.rem(other, bands_n)},
            device_id_type=MESH,
        ).start()
        return carry

    lax.fori_loop(1, group_n, scatter, 0, unroll=group_n <= 16)
    rsbuf[me] = part[me]
    loads["conv1"].wait()
    loads["conv2"].wait()

    def received(i, carry):
        other = lax.rem(me + group_n - i, group_n)
        copy = pltpu.make_async_remote_copy(
            src_ref=part.at[other],
            dst_ref=rsbuf.at[other],
            send_sem=rs_send.at[i],
            recv_sem=rs_recv.at[i],
            device_id={"frames": other // bands_n, "bands": lax.rem(other, bands_n)},
            device_id_type=MESH,
        )
        copy.wait_recv()
        return carry

    lax.fori_loop(1, group_n, received, 0, unroll=group_n <= 16)
    own = jnp.sum(rsbuf[...].astype(F32), 0)
    lat[AGES - 1, reach] = own.astype(BF16)

    offsets = [
        (age, e)
        for age in range(min(AGES, frames_n))
        for e in range(-reach, reach + 1)
        if (age, e) != (0, 0)
    ]

    def hand(age, e):
        return pltpu.make_async_remote_copy(
            src_ref=lat.at[AGES - 1, reach],
            dst_ref=lat.at[AGES - 1 - age, reach - e],
            send_sem=ag_send.at[age, e + reach],
            recv_sem=ag_recv.at[age, e + reach],
            device_id={
                "frames": lax.rem(f + age, frames_n),
                "bands": lax.rem(b + e + bands_n, bands_n),
            },
            device_id_type=MESH,
        )

    def sends(age, e):
        return (f + age < frames_n) & (b + e >= 0) & (b + e < bands_n)

    def takes(age, e):
        return (f - age >= 0) & (b - e >= 0) & (b - e < bands_n)

    for age, e in offsets:

        @pl.when(sends(age, e))
        def _(age=age, e=e):
            hand(age, e).start()

    for age, e in offsets:

        @pl.when(takes(age, e))
        def _(age=age, e=e):
            hand(age, e).wait_recv()

    rows_in = band_rows + 4
    rows_mid = band_rows + 2
    latent = lat[...].astype(F32).reshape(AGES, rows_in, WT, HD)
    flat = latent.reshape(AGES * rows_in * WT, HD)
    mean_square = jnp.mean(flat * flat, -1, keepdims=True)
    normed = flat * lax.rsqrt(mean_square + 1e-06) * gain_ref[...]
    active = (normed * jax.nn.sigmoid(normed)).astype(BF16).astype(F32)
    taps = jnp.concatenate([rolled(active, 1), active, rolled(active, -1)], 1)
    taps = taps.reshape(AGES, rows_in, WT, 3 * HD)
    mid = 3 * rows_mid * WT
    acc = jnp.zeros((mid, HD), F32)
    for i in range(3):
        for j in range(3):
            window = taps[i : i + 3, j : j + rows_mid].reshape(mid, 3 * HD).astype(BF16)
            acc += jnp.dot(window, conv1[i * 3 + j], preferred_element_type=F32)
    centre = latent[2:, 1 : 1 + rows_mid].reshape(mid, HD)
    index = lax.broadcasted_iota(jnp.int32, (mid, HD), 0)
    at_frame = index // (rows_mid * WT) + f - 2
    at_row = index // WT % rows_mid + b * band_rows - 1
    inside = (at_frame >= 0) & (at_row >= 0) & (at_row < bands_n * band_rows)
    hidden = jnp.where(inside, centre + (acc + bias1_ref[...]), 0.0).astype(BF16).astype(F32)
    left, right = rolled(hidden, 1), rolled(hidden, -1)
    sides = [
        jnp.concatenate(list(cols), 1).reshape(3, rows_mid, WT, 3 * HD)
        for cols in ((left, hidden, hidden), (hidden, hidden, right))
    ]
    out_rows = 2 * band_rows
    acc = jnp.zeros((2 * out_rows * WT, HD), F32)
    for i in range(3):
        for j in range(3):
            window = jnp.concatenate(
                [side[i, (y + j + 1) // 2] for side in sides for y in range(out_rows)], 0
            ).astype(BF16)
            acc += jnp.dot(window, conv2[i * 3 + j], preferred_element_type=F32)
    acc = acc + bias2_ref[...]
    for p in range(2):
        for y in range(out_rows):
            first = (p * out_rows + y) * WT
            outf[y, pl.ds(p, WT, 2), :] = acc[first : first + WT]
    out_ref[0] = outf[...].astype(BF16)

    for copy in pending:
        copy.wait_send()

    def sent(i, carry):
        pltpu.make_async_remote_copy(
            src_ref=part.at[lax.rem(me + i, group_n)],
            dst_ref=rsbuf.at[me],
            send_sem=rs_send.at[i],
            recv_sem=rs_recv.at[i],
            device_id={"frames": f, "bands": b},
            device_id_type=MESH,
        ).wait_send()
        return carry

    lax.fori_loop(1, group_n, sent, 0, unroll=group_n <= 16)
    for age, e in offsets:

        @pl.when(sends(age, e))
        def _(age=age, e=e):
            hand(age, e).wait_send()


def local(
    frames_n,
    bands_n,
    span_tokens,
    w_query,
    w_key,
    w_value,
    cache_keys,
    cache_values,
    frame_counts,
    rollback_start,
    w_proj,
    norm_gain,
    conv_first,
    bias_first,
    conv_second,
    bias_second,
):
    _, slot_n, width = span_tokens.shape
    cached_n, _, lw = cache_keys.shape
    rows = cached_n * slot_n
    cw = 256 if lw % 256 == 0 else 128
    chunk_n = lw // cw
    heads = lw // HD
    q_total = frames_n * slot_n
    part_rows = slot_n // bands_n
    band_rows = part_rows // WT
    reach = 2 // band_rows
    key_rows = rows + HD
    group_n = frames_n * bands_n
    anywhere = pl.BlockSpec(memory_space=pl.ANY)
    smem = pl.BlockSpec(memory_space=pltpu.SMEM)
    vmem = pl.BlockSpec(memory_space=pltpu.VMEM)
    dma = pltpu.SemaphoreType.DMA
    return pl.pallas_call(
        functools.partial(kernel, frames_n, bands_n),
        out_shape=pltpu.VMEM((1, 2 * band_rows, 2 * WT, HD), BF16),
        in_specs=[smem, smem] + [anywhere] * 7 + [vmem, anywhere, vmem, anywhere, vmem],
        out_specs=vmem,
        scratch_shapes=[
            pltpu.VMEM((slot_n, width), BF16),
            pltpu.VMEM((chunk_n, width, cw), BF16),
            pltpu.VMEM((chunk_n, width, cw), BF16),
            pltpu.VMEM((chunk_n, width, cw), BF16),
            pltpu.VMEM((key_rows, lw), BF16),
            pltpu.VMEM((key_rows, lw), BF16),
            pltpu.VMEM((lw, HD), BF16),
            pltpu.VMEM((9, 3 * HD, HD), BF16),
            pltpu.VMEM((9, 3 * HD, HD), BF16),
            pltpu.VMEM((chunk_n, frames_n, slot_n, cw), BF16),
            pltpu.VMEM((heads, q_total, key_rows), BF16),
            pltpu.VMEM((heads, q_total, HD), F32),
            pltpu.VMEM((frames_n, 16, q_total), F32),
            pltpu.VMEM((group_n, part_rows, HD), BF16),
            pltpu.VMEM((group_n, part_rows, HD), BF16),
            pltpu.VMEM((AGES, 2 * reach + 1, part_rows, HD), BF16),
            pltpu.VMEM((2 * band_rows, 2 * WT, HD), F32),
            dma((6 + 3 * chunk_n,)),
            dma((chunk_n, frames_n)),
            dma((chunk_n, frames_n)),
            dma((chunk_n, frames_n)),
            dma((chunk_n, frames_n)),
            pltpu.SemaphoreType.REGULAR((2,)),
            dma((frames_n,)),
            dma((frames_n,)),
            dma((group_n,)),
            dma((group_n,)),
            dma((AGES, 2 * reach + 1)),
            dma((AGES, 2 * reach + 1)),
        ],
        compiler_params=pltpu.CompilerParams(
            collective_id=0, has_side_effects=True, vmem_limit_bytes=60 * 1024 * 1024
        ),
    )(
        frame_counts,
        rollback_start,
        span_tokens.reshape(slot_n, width),
        w_query,
        w_key,
        w_value,
        cache_keys.reshape(rows, lw),
        cache_values.reshape(rows, lw),
        w_proj,
        norm_gain.reshape(1, HD),
        conv_first.reshape(9, 3 * HD, HD),
        bias_first.reshape(1, HD),
        conv_second.reshape(9, 3 * HD, HD),
        bias_second.reshape(1, HD),
    )


def solution(mesh):
    placed = (
        P(("groups", "frames"), None, None),
        P(None, "bands"),
        P(None, "bands"),
        P(None, "bands"),
        P(("groups", "frames"), None, "bands"),
        P(("groups", "frames"), None, "bands"),
        P(("groups", "frames")),
        P("groups"),
        P("bands", None),
        P(),
        P(),
        P(),
        P(),
        P(),
    )
    return jax.shard_map(
        functools.partial(local, mesh.shape["frames"], mesh.shape["bands"]),
        mesh=mesh,
        in_specs=placed,
        out_specs=P(("groups", "frames"), "bands", None, None),
        check_vma=False,
    )
```
